128 devices in a mesh: row: 4 (over z), col: 16 (over y, x_lo, core), depth: 2 (over x_hi).
Axes of the slice: x: 4 (x_hi: 2, x_lo: 2; x = x_hi * 2 + x_lo), y: 4, z: 4, core: 2. Of those that a mesh axis runs over, the one named last changes fastest.
Arguments:
- layer_input: bfloat16 [1536, 6144], P(('depth', 'col'), 'row'), may hold values from -6 to 6
- w_in: bfloat16 [6144, 24576], P('row', 'col'), may hold values from -0.078125 to 0.078125
- w_out: bfloat16 [24576, 6144], P('col', 'row'), may hold values from -0.0390625 to 0.0390625
- out_grad: bfloat16 [1536, 6144], P(('depth', 'col'), 'row'), may hold values from -0.95703125 to 0.95703125
- drop_seed: int32 [1], replicated, may hold values from 0 to 1073741823
- drop_step: int32 [1], replicated, may hold values from 0 to 999999
Outputs:
- input_grad: float32 [1536, 6144], P(('depth', 'col'), 'row')
- w_in_grad: float32 [6144, 24576], P('row', ('col', 'depth'))
- w_out_grad: float32 [24576, 6144], P('col', ('row', 'depth'))
The draws below stay inside these ranges and needn't reach their ends.
All inputs are finite; a program needn't handle non-finite values.
Results may differ from the reference program's by a relative error of at most 0.0041.
Values may be sent and summed in bfloat16 or wider, within the bound.
A program may use at most 128 MiB of HBM per device.

```python
import math
import jax
import jax.numpy as jnp
from jax import lax

D = 6144
FF = 24576
TOKENS = 1536


def levels(rng, extent, pieces, smallest, largest):
    gain, own = 1.0, jax.random.fold_in(rng, 6)
    for axis_at, blocks in pieces:
        steps = jnp.exp(jax.random.uniform(jax.random.fold_in(own, axis_at), (blocks,), jnp.float32, smallest / len(pieces), largest / len(pieces)))
        gain = gain * jnp.repeat(steps, extent[axis_at] // blocks).reshape([-1 if axis == axis_at else 1 for axis in range(len(extent))])
    return gain


def noise(own_key, extent, deviation, reach, cuts=(), held_as=jnp.bfloat16):
    result = deviation * jax.random.normal(own_key, extent, jnp.float32)
    if cuts:
        result = result * levels(own_key, extent, cuts, -0.22, 0.18)
    return jnp.clip(result, -reach, reach).astype(held_as)


def setup_inputs(seed: int = 0) -> dict:
    splits = jax.random.split(jax.random.key(seed), 7)
    return {
        "layer_input": noise(splits[0], (TOKENS, D), 1.0, 6.0, ((0, 32), (1, 4))),
        "w_in": noise(splits[1], (D, FF), D ** -0.5, 0.078125, ((0, 4), (1, 16))),
        "w_out": noise(splits[2], (FF, D), FF ** -0.5, 0.0390625, ((0, 16), (1, 4))),
        "out_grad": noise(splits[3], (TOKENS, D), (TOKENS ** -0.25), 0.95703125, ((0, 32), (1, 4))),
        "drop_seed": jax.random.randint(splits[4], (1,), 0, 1073741824).astype(jnp.int32),
        "drop_step": jax.random.randint(splits[5], (1,), 0, 1000000).astype(jnp.int32),
    }


keep_scale = 1.0 / 0.9
gelu_coef = math.sqrt(2.0 / math.pi)

def mix_bits(word_bits):
    word_bits = word_bits ^ lax.shift_right_logical(word_bits, jnp.int32(16))
    word_bits = word_bits * jnp.int32(2146121005)
    word_bits = word_bits ^ lax.shift_right_logical(word_bits, jnp.int32(15))
    word_bits = word_bits * jnp.int32(-2073254261)
    word_bits = word_bits ^ lax.shift_right_logical(word_bits, jnp.int32(16))
    return word_bits

def keep_mask(drop_seed, drop_step, row_start, col_start, row_count, col_count, row_length):
    stream_key = mix_bits(mix_bits(drop_step[0] + jnp.int32(1013904223)) ^ drop_seed[0])
    row_ids = jnp.arange(row_count, dtype=jnp.int32) + row_start
    col_ids = jnp.arange(col_count, dtype=jnp.int32) + col_start
    flat_index = row_ids[:, None] * jnp.int32(row_length) + col_ids[None, :]
    hashed = mix_bits(flat_index ^ stream_key)
    return hashed & jnp.int32(16777215) < jnp.int32(15099494)

def gelu_parts(hidden_pre):
    inner_arg = gelu_coef * (hidden_pre + 0.044715 * hidden_pre * hidden_pre * hidden_pre)
    tanh_val = jnp.tanh(inner_arg)
    act_full = 0.5 * hidden_pre * (1.0 + tanh_val)
    gelu_slope = 0.5 * (1.0 + tanh_val) + 0.5 * hidden_pre * (1.0 - tanh_val * tanh_val) * gelu_coef * (1.0 + 3.0 * 0.044715 * hidden_pre * hidden_pre)
    return (act_full, gelu_slope)

def reference(layer_input, w_in, w_out, out_grad, drop_seed, drop_step):
    hidden_pre = jnp.dot(layer_input, w_in, preferred_element_type=jnp.float32)
    act_full, gelu_slope = gelu_parts(hidden_pre)
    hidden_act = act_full.astype(jnp.bfloat16)
    keep_flags = keep_mask(drop_seed, drop_step, jnp.int32(0), jnp.int32(0), TOKENS, D, D)
    scaled = jnp.where(keep_flags, out_grad.astype(jnp.float32) * keep_scale, jnp.zeros((), jnp.float32)).astype(jnp.bfloat16)
    act_grad = lax.dot_general(scaled, w_out, (((1,), (1,)), ((), ())), preferred_element_type=jnp.float32)
    pre_grad = (act_grad * gelu_slope).astype(jnp.bfloat16)
    w_out_grad = lax.dot_general(hidden_act, scaled, (((0,), (0,)), ((), ())), preferred_element_type=jnp.float32)
    w_in_grad = lax.dot_general(layer_input, pre_grad, (((0,), (0,)), ((), ())), preferred_element_type=jnp.float32)
    input_grad = lax.dot_general(pre_grad, w_in, (((1,), (1,)), ((), ())), preferred_element_type=jnp.float32)
    return (input_grad, w_in_grad, w_out_grad)
```

```python
import math

import jax
import jax.numpy as jnp
from jax import lax
from jax.experimental import pallas as pl
from jax.experimental.pallas import tpu as pltpu
from jax.sharding import PartitionSpec as P

D = 6144
keep_scale = 1.0 / 0.9
gelu_coef = math.sqrt(2.0 / math.pi)
F32, BF16, I32 = jnp.float32, jnp.bfloat16, jnp.int32
MESH = pl.DeviceIdType.MESH

OWN = 48
CH = 384
QT = 96
HID = 768
FEAT = 1536
ITEMS = [(0, 0), (0, 1), (0, 3), (0, 2), (1, 2), (1, 1), (1, 3), (1, 0)]
N_SEMS = 400

NN = (((1,), (0,)), ((), ()))
NT = (((1,), (1,)), ((), ()))


def mix_bits(v):
    v = v ^ lax.shift_right_logical(v, jnp.int32(16))
    v = v * jnp.int32(2146121005)
    v = v ^ lax.shift_right_logical(v, jnp.int32(15))
    v = v * jnp.int32(-2073254261)
    v = v ^ lax.shift_right_logical(v, jnp.int32(16))
    return v


def gelu_parts(h):
    inner_arg = gelu_coef * (h + 0.044715 * h * h * h)
    t = jnp.tanh(inner_arg)
    act = 0.5 * h * (1.0 + t)
    slope = 0.5 * (1.0 + t) + 0.5 * h * (1.0 - t * t) * gelu_coef * (1.0 + 3.0 * 0.044715 * h * h)
    return act, slope


def slot(b, region, a):
    return pl.ds(((b * 2 + region) * 4 + a) * OWN, OWN)


def kernel(
    x_hbm, win_hbm, wout_hbm, og_hbm, seed_ref, step_ref,
    ig_hbm, wing_hbm, woutg_hbm,
    X, S, XT, HT, H, G, WI, WO, OG,
    PF, PB, RU, RD, C1, C2, FB, FA, SL,
    Q32, R32, CS, CR, QS, RLU, RLD, RB, FS, FR, IG,
    WS, WRU, WRD, WR, OUT,
    sems, lsem, osem,
):
    z = lax.axis_index("row")
    col = lax.axis_index("col")
    d = lax.axis_index("depth")
    core = lax.rem(col, 2)
    x = d * 2 + lax.rem(lax.div(col, 2), 2)
    y = lax.div(col, 4)

    def dev(xx, yy, zz, cc):
        xx, yy, zz = lax.rem(xx, 4), lax.rem(yy, 4), lax.rem(zz, 4)
        return {"row": zz, "col": yy * 4 + lax.rem(xx, 2) * 2 + cc, "depth": lax.div(xx, 2)}

    def first(k):
        return dev(x + k * (1 - core), y + k * core, z, core)

    def second(k):
        return dev(x + k * core, y + k * (1 - core), z, core)

    zup, zdn = dev(x, y, z + 1, core), dev(x, y, z + 3, core)
    xup, xdn = dev(x + 1, y, z, core), dev(x + 3, y, z, core)
    mate = dev(x, y, z, 1 - core)

    started = []

    def send(src, dst, to):
        k = 2 * len(started)
        copy = pltpu.make_async_remote_copy(
            src_ref=src, dst_ref=dst, send_sem=sems.at[k], recv_sem=sems.at[k + 1],
            device_id=to, device_id_type=MESH,
        )
        copy.start()
        started.append(copy)
        return copy

    def load(src, dst, k):
        c = pltpu.make_async_copy(src, dst, lsem.at[k])
        c.start()
        return c

    own = slot(0, 0, 0)
    half = pl.ds(pl.multiple_of(d * HID, HID), HID)
    other = pl.ds(pl.multiple_of((1 - d) * HID, HID), HID)
    ld_x = load(x_hbm, X.at[own, :], 0)
    ld_g = load(og_hbm, OG, 1)
    ld_wi = load(win_hbm.at[:, half], WI, 2)
    ld_wo = load(wout_hbm.at[half, :], WO, 3)

    barrier = pltpu.get_barrier_semaphore()
    near = [first(1), first(3), first(2), second(1), second(3), zup, zdn, mate]
    for n in near:
        pl.semaphore_signal(barrier, inc=1, device_id=n, device_id_type=MESH)
    pl.semaphore_wait(barrier, len(near))

    LH, RH = pl.ds(0, 768), pl.ds(768, 768)

    class Gather:
        def __init__(self, buf):
            self.buf = buf
            self.c = {}

        def spread(self, a):
            sl = self.buf.at[slot(0, 0, a), :]
            self.c[a, 1] = send(sl, self.buf.at[slot(1, 0, a), :], second(1))
            self.c[a, 3] = send(sl, self.buf.at[slot(3, 0, a), :], second(3))
            self.share(a, 0)

        def share(self, a, b):
            self.c["m", a, b] = send(self.buf.at[slot(b, 0, a), :], self.buf.at[slot(b, 1, a), :], mate)

        def begin(self):
            sl = self.buf.at[own, :]
            self.f1 = send(sl, self.buf.at[slot(0, 0, 1), :], first(1))
            self.f3 = send(sl, self.buf.at[slot(0, 0, 3), :], first(3))
            self.spread(0)

        def firsts(self):
            self.f1.wait_recv()
            l = send(self.buf.at[slot(0, 0, 1), LH], self.buf.at[slot(0, 0, 2), LH], first(1))
            self.spread(1)
            self.f3.wait_recv()
            r = send(self.buf.at[slot(0, 0, 3), RH], self.buf.at[slot(0, 0, 2), RH], first(3))
            self.spread(3)
            l.wait_recv()
            r.wait_recv()
            self.spread(2)

        def seconds(self, a):
            self.c[a, 1].wait_recv()
            self.c[a, "l"] = send(self.buf.at[slot(1, 0, a), LH], self.buf.at[slot(2, 0, a), LH], second(1))
            self.share(a, 1)
            self.c[a, 3].wait_recv()
            self.c[a, "r"] = send(self.buf.at[slot(3, 0, a), RH], self.buf.at[slot(2, 0, a), RH], second(3))
            self.share(a, 3)

        def thirds(self):
            for a in (0, 1, 3, 2):
                self.c[a, "l"].wait_recv()
                self.c[a, "r"].wait_recv()
                self.share(a, 2)

        def ready(self, b):
            for a in (0, 1, 3, 2):
                shared = self.c.pop(("m", a, b), None)
                if shared is not None:
                    shared.wait_recv()

    gx, gs = Gather(X), Gather(S)

    def mul(n):
        return pl.multiple_of(n * 256, 256)

    st = {}
    AL, AR = pl.ds(0, 384), pl.ds(384, 384)

    def quarter(k):
        return pl.ds(pl.multiple_of(lax.rem(z + k, 4) * QT, QT), QT)

    def s0(i):
        q, b = ITEMS[i]
        pf, pb = PF.at[i % 2], PB.at[i]
        rows = pl.ds(b * CH, CH)
        (gs if q else gx).ready(b)

        @pl.loop(0, 3)
        def _(n):
            cols = pl.ds(mul(n), 256)
            if q:
                r = lax.dot_general(S[rows, :], WO[cols, :], NT, preferred_element_type=F32)
            else:
                r = lax.dot_general(X[rows, :], WI[:, cols], NN, preferred_element_type=F32)
            pf[:, cols] = r
            pb[:, cols] = r.astype(BF16)

        st[i, "a1"] = send(pb.at[quarter(2), AL], RU.at[i], zup)
        st[i, "a2"] = send(pb.at[quarter(2), AR], RD.at[i], zdn)
        st[i, "b1"] = send(pb.at[quarter(1), AR], FB.at[i, :, AR], zup)
        st[i, "b2"] = send(pb.at[quarter(3), AL], FA.at[i, :, AL], zdn)

    def s1(i):
        pf = PF.at[i % 2]

        def add(relay, out, k, cols):
            base = lax.rem(z + k, 4) * QT

            @pl.loop(0, QT // 32)
            def _(j):
                o = pl.multiple_of(j * 32, 32)
                src = pl.ds(pl.multiple_of(base + o, 32), 32)
                out[pl.ds(o, 32), :] = (relay[pl.ds(o, 32), :].astype(F32) + pf[src, cols]).astype(BF16)

        st[i, "a1"].wait_recv()
        add(RU.at[i], C1.at[i], 1, AL)
        st[i, "c1"] = send(C1.at[i], FB.at[i, :, AL], zup)
        st[i, "a2"].wait_recv()
        add(RD.at[i], C2.at[i], 3, AR)
        st[i, "c2"] = send(C2.at[i], FA.at[i, :, AR], zdn)

    def s2(i):
        q, b = ITEMS[i]
        pf = PF.at[i % 2]
        for k in ("b1", "b2", "c1", "c2"):
            st[i, k].wait_recv()
        dst = G if q else H
        row0 = b * CH + z * QT

        @pl.loop(0, QT // 16)
        def _(j):
            o = pl.multiple_of(j * 16, 16)
            rr = pl.ds(o, 16)
            src = pl.ds(pl.multiple_of(z * QT + o, 16), 16)
            to = pl.ds(pl.multiple_of(row0 + o, 16), 16)
            v = pf[src, :] + FB[i, rr, :].astype(F32) + FA[i, rr, :].astype(F32)
            if q:
                dst[to, :] = (v * SL[b, rr, :]).astype(BF16)
            else:
                act, slope = gelu_parts(v)
                dst[to, :] = act.astype(BF16)
                SL[b, rr, :] = slope

        mine = dst.at[pl.ds(pl.multiple_of(row0, 16), QT), :]
        st[i, "n1"] = send(mine, mine, zup)
        st[i, "n2"] = send(mine, mine, zdn)

    def s3(i):
        q, b = ITEMS[i]
        dst = G if q else H
        up = pl.ds(pl.multiple_of(b * CH + lax.rem(z + 3, 4) * QT, 16), QT)
        dn = pl.ds(pl.multiple_of(b * CH + lax.rem(z + 1, 4) * QT, 16), QT)
        st[i, "n1"].wait_recv()
        st[i, "w1"] = send(dst.at[up, AL], dst.at[up, AL], zup)
        st[i, "n2"].wait_recv()
        st[i, "w2"] = send(dst.at[dn, AR], dst.at[dn, AR], zdn)

    def flip(src, dst, b, width):
        @pl.loop(0, width // 128)
        def _(n):
            c = pl.ds(pl.multiple_of(n * 128, 128), 128)
            dst[c, pl.ds(b * CH, CH)] = src[pl.ds(b * CH, CH), c].T

    def s4(i):
        q, b = ITEMS[i]
        st[i, "w1"].wait_recv()
        st[i, "w2"].wait_recv()
        if not q:
            flip(H, HT, b, HID)
            return
        cs = CS.at[b]

        @pl.loop(0, 6)
        def _(n):
            cols = pl.ds(mul(n), 256)
            r = lax.dot_general(G[pl.ds(b * CH, CH), :], WI[cols, :], NT, preferred_element_type=F32)
            Q32[:, cols] = r[0:192]
            cs[:, cols] = r[192:384].astype(BF16)

        st[i, "m"] = send(cs, CR.at[b], mate)

    def s5(i):
        _, b = ITEMS[i]
        st[i, "m"].wait_recv()

        @pl.loop(0, 12)
        def _(j):
            rr = pl.ds(pl.multiple_of(j * 16, 16), 16)
            v = Q32[rr, :] + CR[b, rr, :].astype(F32)
            if b:
                QS[b - 1, rr, :] = v.astype(BF16)
            else:
                R32[rr, :] = v

        if b == 1:
            st["r1"] = send(QS.at[0], RB.at[0], second(3))
        elif b == 3:
            st["r3"] = send(QS.at[2], RB.at[2], second(1))
        elif b == 2:
            st["rl"] = send(QS.at[1, :, LH], RLU, second(1))
            st["rr"] = send(QS.at[1, :, RH], RLD, second(3))

    def relay_two():
        st["rl"].wait_recv()
        st["r2l"] = send(RLU, RB.at[1, :, LH], second(1))
        st["rr"].wait_recv()
        st["r2r"] = send(RLD, RB.at[1, :, RH], second(3))

    outs = {}

    def put(k, dst):
        c = pltpu.make_async_copy(OUT.at[k % 2], dst, osem.at[k])
        c.start()
        outs[k] = c

    def w_out_away():
        @pl.loop(0, 6)
        def _(t):
            m, n = lax.div(t, 3), lax.rem(t, 3)
            rows = pl.ds(pl.multiple_of(m * 384, 384), 384)
            cols = pl.ds(pl.multiple_of((1 - d) * HID + n * 256, 256), 256)
            r = lax.dot_general(HT[rows, :], S[:, cols], NN, preferred_element_type=F32)
            WS[rows, pl.ds(mul(n), 256)] = r.astype(BF16)

        st["s1"] = send(WS.at[pl.ds(0, 384), :], WRU, xup)
        st["s2"] = send(WS.at[pl.ds(384, 384), :], WRD, xdn)

    def w_out_home(m):
        @pl.loop(0, 3)
        def _(n):
            cols = pl.ds(pl.multiple_of(d * HID + n * 256, 256), 256)
            r = lax.dot_general(HT[pl.ds(m * 384, 384), :], S[:, cols], NN, preferred_element_type=F32)
            OUT[m, :, pl.ds(mul(n), 256)] = r

        put(m, woutg_hbm.at[pl.ds(pl.multiple_of(d * HID + m * 384, 384), 384), :])

    def relay_swap():
        st["s1"].wait_recv()
        st["t1"] = send(WRU, WR.at[pl.ds(0, 384), :], xup)
        st["s2"].wait_recv()
        st["t2"] = send(WRD, WR.at[pl.ds(384, 384), :], xdn)

    def w_out_far(m):
        st["t%d" % (m + 1)].wait_recv()
        outs[m].wait()

        @pl.loop(0, 12)
        def _(j):
            o = pl.multiple_of(j * 32, 32)
            OUT[m, pl.ds(o, 32), :] = WR[pl.ds(pl.multiple_of(m * 384 + o, 32), 32), :].astype(F32)

        put(2 + m, woutg_hbm.at[pl.ds(pl.multiple_of((1 - d) * HID + m * 384, 384), 384), :])

    def w_in_part(m):
        outs[2 + m].wait()

        @pl.loop(0, 3)
        def _(n):
            cols = pl.ds(mul(n), 256)
            OUT[m % 2, :, cols] = lax.dot_general(
                XT[pl.ds(m * 384, 384), :], G[:, cols], NN, preferred_element_type=F32
            )

        put(4 + m, wing_hbm.at[pl.ds(m * 384, 384), :])

    ld_x.wait()
    gx.begin()
    ld_g.wait()
    key = mix_bits(mix_bits(step_ref[0] + jnp.int32(1013904223)) ^ seed_ref[0])
    row0 = (d * 16 + col) * OWN

    @pl.loop(0, OWN // 16)
    def _(j):
        rr = pl.ds(pl.multiple_of(j * 16, 16), 16)
        rows = lax.broadcasted_iota(I32, (16, FEAT), 0) + (row0 + j * 16)
        cols = lax.broadcasted_iota(I32, (16, FEAT), 1) + z * FEAT
        hashed = mix_bits((rows * jnp.int32(D) + cols) ^ key)
        keep = (hashed & jnp.int32(16777215)) < jnp.int32(15099494)
        v = jnp.where(keep, OG[rr, :].astype(F32) * keep_scale, jnp.zeros((), F32))
        S[rr, :] = v.astype(BF16)

    gx.firsts()
    ld_wi.wait()
    s0(0)
    gx.seconds(0)
    gx.seconds(1)
    s1(0)
    gx.seconds(3)
    gx.seconds(2)
    s0(1)
    s2(0)
    gs.begin()
    s1(1)
    gx.thirds()
    gs.firsts()
    s3(0)
    s0(2)
    s2(1)
    s1(2)
    s4(0)
    gs.seconds(0)
    gs.seconds(1)
    s3(1)
    s0(3)
    s2(2)
    s1(3)
    s4(1)
    gs.seconds(3)
    gs.seconds(2)
    s3(2)
    gs.thirds()
    ld_wo.wait()
    s0(4)
    s2(3)
    s1(4)
    s4(2)
    flip(X, XT, 0, FEAT)
    s3(3)
    s0(5)
    s2(4)
    s1(5)
    s4(3)
    gs.ready(0)
    gs.ready(3)
    w_out_away()
    s3(4)
    s0(6)
    s2(5)
    s1(6)
    s4(4)
    w_out_home(0)
    w_out_home(1)
    s3(5)
    s0(7)
    s2(6)
    s1(7)
    s5(4)
    s4(5)
    relay_swap()
    flip(X, XT, 1, FEAT)
    s3(6)
    s2(7)
    s5(5)
    s4(6)
    relay_two()
    s5(6)
    flip(X, XT, 3, FEAT)
    flip(X, XT, 2, FEAT)
    s3(7)
    s4(7)
    w_out_far(0)
    w_out_far(1)
    w_in_part(0)
    s5(7)
    for k in ("r1", "r2l", "r2r", "r3"):
        st[k].wait_recv()

    @pl.loop(0, 12)
    def _(j):
        rr = pl.ds(pl.multiple_of(j * 16, 16), 16)
        v = R32[rr, :] + RB[0, rr, :].astype(F32) + RB[1, rr, :].astype(F32) + RB[2, rr, :].astype(F32)
        R32[rr, :] = v
        FS[rr, :] = v.astype(BF16)

    st["f1"] = send(FS.at[pl.ds(OWN, OWN), :], FR.at[0], first(3))
    st["f2"] = send(FS.at[pl.ds(2 * OWN, OWN), :], FR.at[1], first(2))
    st["f3"] = send(FS.at[pl.ds(3 * OWN, OWN), :], FR.at[2], first(1))
    w_in_part(1)
    w_in_part(2)
    w_in_part(3)
    for k in ("f1", "f2", "f3"):
        st[k].wait_recv()

    @pl.loop(0, OWN // 16)
    def _(j):
        rr = pl.ds(pl.multiple_of(j * 16, 16), 16)
        IG[rr, :] = (
            R32[rr, :] + FR[0, rr, :].astype(F32) + FR[1, rr, :].astype(F32) + FR[2, rr, :].astype(F32)
        )

    fin = pltpu.make_async_copy(IG, ig_hbm, osem.at[8])
    fin.start()
    fin.wait()
    outs[6].wait()
    outs[7].wait()
    for copy in started:
        copy.wait_send()


def per_device(layer_input, w_in, w_out, out_grad, drop_seed, drop_step):
    hbm = pl.BlockSpec(memory_space=pl.ANY)
    smem = pl.BlockSpec(memory_space=pltpu.SMEM)

    def b(*shape):
        return pltpu.VMEM(shape, BF16)

    def f(*shape):
        return pltpu.VMEM(shape, F32)

    return pl.pallas_call(
        kernel,
        out_shape=(
            jax.ShapeDtypeStruct((OWN, FEAT), F32),
            jax.ShapeDtypeStruct((FEAT, HID), F32),
            jax.ShapeDtypeStruct((2 * HID, HID), F32),
        ),
        in_specs=[hbm, hbm, hbm, hbm, smem, smem],
        out_specs=(hbm, hbm, hbm),
        scratch_shapes=[
            b(1536, FEAT), b(1536, FEAT), b(FEAT, 1536), b(HID, 1536), b(1536, HID), b(1536, HID),
            b(FEAT, HID), b(HID, FEAT), b(OWN, FEAT),
            f(2, CH, HID), b(8, CH, HID), b(8, QT, 384), b(8, QT, 384), b(8, QT, 384), b(8, QT, 384),
            b(8, QT, HID), b(8, QT, HID), f(4, QT, HID),
            f(192, FEAT), f(192, FEAT), b(4, 192, FEAT), b(4, 192, FEAT), b(3, 192, FEAT),
            b(192, 768), b(192, 768), b(3, 192, FEAT), b(192, FEAT), b(3, OWN, FEAT), f(OWN, FEAT),
            b(HID, HID), b(384, HID), b(384, HID), b(HID, HID), f(2, 384, HID),
            pltpu.SemaphoreType.DMA((N_SEMS,)),
            pltpu.SemaphoreType.DMA((4,)),
            pltpu.SemaphoreType.DMA((9,)),
        ],
        compiler_params=pltpu.CompilerParams(
            collective_id=0, has_side_effects=True, vmem_limit_bytes=67_000_000
        ),
        name="mlp_backward",
    )(layer_input, w_in, w_out, out_grad, drop_seed, drop_step)


def solution(mesh):
    placed = (
        P(("depth", "col"), "row"),
        P("row", "col"),
        P("col", "row"),
        P(("depth", "col"), "row"),
        P(),
        P(),
    )
    return jax.shard_map(
        per_device,
        mesh=mesh,
        in_specs=placed,
        out_specs=(
            P(("depth", "col"), "row"),
            P("row", ("col", "depth")),
            P("col", ("row", "depth")),
        ),
        check_vma=False,
    )
```

```python
import math

import jax
import jax.numpy as jnp
from jax import lax
from jax.experimental import pallas as pl
from jax.experimental.pallas import tpu as pltpu
from jax.sharding import PartitionSpec as P

D = 6144
keep_scale = 1.0 / 0.9
gelu_coef = math.sqrt(2.0 / math.pi)
F32, BF16, I32 = jnp.float32, jnp.bfloat16, jnp.int32
MESH = pl.DeviceIdType.MESH

OWN = 48
CH = 384
QT = 96
HID = 768
FEAT = 1536
ITEMS = [
    (0, 0, 0, 0), (0, 0, 1, 0), (0, 1, None, 1), (0, 3, None, 2), (0, 2, None, 3),
    (1, 1, None, 4), (1, 2, None, 5), (1, 3, None, 6), (1, 0, 1, 7), (1, 0, 0, 7),
]
POS = (0, 2, 1, 3)
N_SEMS = 400

NN = (((1,), (0,)), ((), ()))
NT = (((1,), (1,)), ((), ()))


def mix_bits(v):
    v = v ^ lax.shift_right_logical(v, jnp.int32(16))
    v = v * jnp.int32(2146121005)
    v = v ^ lax.shift_right_logical(v, jnp.int32(15))
    v = v * jnp.int32(-2073254261)
    v = v ^ lax.shift_right_logical(v, jnp.int32(16))
    return v


def gelu_parts(h):
    inner_arg = gelu_coef * (h + 0.044715 * h * h * h)
    t = jnp.tanh(inner_arg)
    act = 0.5 * h * (1.0 + t)
    slope = 0.5 * (1.0 + t) + 0.5 * h * (1.0 - t * t) * gelu_coef * (1.0 + 3.0 * 0.044715 * h * h)
    return act, slope


def slot(b, region, a):
    return pl.ds(((b * 2 + region) * 4 + POS[a]) * OWN, OWN)


def kernel(
    x_hbm, win_hbm, wout_hbm, og_hbm, seed_ref, step_ref,
    ig_hbm, wing_hbm, woutg_hbm,
    X, S, XT, HT, H, G, WI, WO, OG,
    PF, PB, RU, RD, C1, C2, FB, FA, SL,
    Q32, QO, CS, CR, QS, RA, QB, RB, IG,
    WS, WRU, WRD, WR, OUT, WG,
    sems, lsem, osem,
):
    z = lax.axis_index("row")
    col = lax.axis_index("col")
    d = lax.axis_index("depth")
    core = lax.rem(col, 2)
    x = d * 2 + lax.rem(lax.div(col, 2), 2)
    y = lax.div(col, 4)

    def dev(xx, yy, zz, cc):
        xx, yy, zz = lax.rem(xx, 4), lax.rem(yy, 4), lax.rem(zz, 4)
        return {"row": zz, "col": yy * 4 + lax.rem(xx, 2) * 2 + cc, "depth": lax.div(xx, 2)}

    def first(k):
        return dev(x + k * (1 - core), y + k * core, z, core)

    def second(k):
        return dev(x + k * core, y + k * (1 - core), z, core)

    zup, zdn = dev(x, y, z + 1, core), dev(x, y, z + 3, core)
    xup, xdn = dev(x + 1, y, z, core), dev(x + 3, y, z, core)
    mate = dev(x, y, z, 1 - core)

    started = []

    def send(src, dst, to):
        k = 2 * len(started)
        copy = pltpu.make_async_remote_copy(
            src_ref=src, dst_ref=dst, send_sem=sems.at[k], recv_sem=sems.at[k + 1],
            device_id=to, device_id_type=MESH,
        )
        copy.start()
        started.append(copy)
        return copy

    def load(src, dst, k):
        c = pltpu.make_async_copy(src, dst, lsem.at[k])
        c.start()
        return c

    own = slot(0, 0, 0)
    half = pl.ds(pl.multiple_of(d * HID, HID), HID)
    other = pl.ds(pl.multiple_of((1 - d) * HID, HID), HID)
    ld_x = load(x_hbm, X.at[own, :], 0)
    ld_g = load(og_hbm, OG, 1)
    ld_wi = load(win_hbm.at[:, half], WI, 2)
    ld_wo = load(wout_hbm.at[half, :], WO, 3)

    barrier = pltpu.get_barrier_semaphore()
    near = [first(1), first(3), first(2), second(1), second(3), second(2), zup, zdn, mate]
    for n in near:
        pl.semaphore_signal(barrier, inc=1, device_id=n, device_id_type=MESH)
    pl.semaphore_wait(barrier, len(near))

    LH, RH = pl.ds(0, 768), pl.ds(768, 768)

    class Gather:
        def __init__(self, buf):
            self.buf = buf
            self.c = {}

        def spread(self, a):
            sl = self.buf.at[slot(0, 0, a), :]
            self.c[a, 1] = send(sl, self.buf.at[slot(1, 0, a), :], second(1))
            self.c[a, 3] = send(sl, self.buf.at[slot(3, 0, a), :], second(3))

        def share(self, a, b):
            self.c["m", a, b] = send(self.buf.at[slot(b, 0, a), :], self.buf.at[slot(b, 1, a), :], mate)

        def begin(self):
            sl = self.buf.at[own, :]
            self.f1 = send(sl, self.buf.at[slot(0, 0, 1), :], first(1))
            self.f3 = send(sl, self.buf.at[slot(0, 0, 3), :], first(3))
            self.share(0, 0)

        def firsts(self):
            self.f1.wait_recv()
            l = send(self.buf.at[slot(0, 0, 1), LH], self.buf.at[slot(0, 0, 2), LH], first(1))
            self.share(1, 0)
            self.f3.wait_recv()
            r = send(self.buf.at[slot(0, 0, 3), RH], self.buf.at[slot(0, 0, 2), RH], first(3))
            self.share(3, 0)
            for a in (0, 1, 3):
                self.spread(a)
            self.l, self.r = l, r

        def firsts_two(self):
            self.l.wait_recv()
            self.r.wait_recv()
            self.share(2, 0)
            self.spread(2)

        def seconds(self, a):
            self.c[a, 1].wait_recv()
            self.c[a, "l"] = send(self.buf.at[slot(1, 0, a), LH], self.buf.at[slot(2, 0, a), LH], second(1))
            self.share(a, 1)
            self.c[a, 3].wait_recv()
            self.c[a, "r"] = send(self.buf.at[slot(3, 0, a), RH], self.buf.at[slot(2, 0, a), RH], second(3))
            self.share(a, 3)

        def thirds(self):
            for a in (0, 1, 3, 2):
                self.c[a, "l"].wait_recv()
                self.c[a, "r"].wait_recv()
                self.share(a, 2)

        def ready(self, b, slots=(0, 1, 3, 2)):
            for a in slots:
                shared = self.c.pop(("m", a, b), None)
                if shared is not None:
                    shared.wait_recv()

    gx, gs = Gather(X), Gather(S)

    def mul(n):
        return pl.multiple_of(n * 256, 256)

    st = {}
    AL, AR = pl.ds(0, 384), pl.ds(384, 384)

    def shape(i):
        _, b, part, k = ITEMS[i]
        rows = QT if part is None else OWN
        return b, k, rows, (part or 0) * OWN

    def quarter(k, rows):
        return pl.multiple_of(lax.rem(z + k, 4) * rows, 16)

    def tokens(buf, i, cols=None):
        b, _, rows, off = shape(i)
        if rows == QT:
            return buf[pl.ds(b * CH, CH), :]
        return jnp.concatenate([buf[pl.ds(b * CH + g * QT + off, OWN), :] for g in range(4)], axis=0)

    def s0(i):
        q = ITEMS[i][0]
        b, k, rows, off = shape(i)
        base = off * 4
        pf, pb = PF.at[i % 2], PB.at[k]
        (gs if q else gx).ready(b, (0, 1, 3, 2) if rows == QT else ((2, 3) if off else (0, 1)))

        @pl.loop(0, 3)
        def _(n):
            cols = pl.ds(mul(n), 256)
            if q:
                r = lax.dot_general(tokens(S, i), WO[cols, :], NT, preferred_element_type=F32)
            else:
                r = lax.dot_general(tokens(X, i), WI[:, cols], NN, preferred_element_type=F32)
            pf[pl.ds(0, 4 * rows), cols] = r
            pb[pl.ds(base, 4 * rows), cols] = r.astype(BF16)

        def part(j):
            return pl.ds(base + quarter(j, rows), rows)

        mine = pl.ds(off, rows)
        st[i, "a1"] = send(pb.at[part(2), AL], RU.at[k, mine], zup)
        st[i, "a2"] = send(pb.at[part(2), AR], RD.at[k, mine], zdn)
        st[i, "b1"] = send(pb.at[part(1), AR], FB.at[k, mine, AR], zup)
        st[i, "b2"] = send(pb.at[part(3), AL], FA.at[k, mine, AL], zdn)

    def s1(i):
        _, k, rows, off = shape(i)
        pf = PF.at[i % 2]
        mine = pl.ds(off, rows)

        def add(relay, out, j, cols):
            base = quarter(j, rows)

            @pl.loop(0, rows // 16)
            def _(t):
                o = pl.multiple_of(t * 16, 16)
                rr = pl.ds(off + o, 16)
                src = pl.ds(pl.multiple_of(base + o, 16), 16)
                out[rr, :] = (relay[rr, :].astype(F32) + pf[src, cols]).astype(BF16)

        st[i, "a1"].wait_recv()
        add(RU.at[k], C1.at[k], 1, AL)
        st[i, "c1"] = send(C1.at[k, mine], FB.at[k, mine, AL], zup)
        st[i, "a2"].wait_recv()
        add(RD.at[k], C2.at[k], 3, AR)
        st[i, "c2"] = send(C2.at[k, mine], FA.at[k, mine, AR], zdn)

    def s2(i):
        q = ITEMS[i][0]
        b, k, rows, off = shape(i)
        pf = PF.at[i % 2]
        for key in ("b1", "b2", "c1", "c2"):
            st[i, key].wait_recv()
        dst = G if q else H
        row0 = b * CH + z * QT + off
        base = quarter(0, rows)

        @pl.loop(0, rows // 16)
        def _(t):
            o = pl.multiple_of(t * 16, 16)
            rr = pl.ds(off + o, 16)
            src = pl.ds(pl.multiple_of(base + o, 16), 16)
            to = pl.ds(pl.multiple_of(row0 + o, 16), 16)
            v = pf[src, :] + FB[k, rr, :].astype(F32) + FA[k, rr, :].astype(F32)
            if q:
                dst[to, :] = (v * SL[b, rr, :]).astype(BF16)
            else:
                act, slope = gelu_parts(v)
                dst[to, :] = act.astype(BF16)
                SL[b, rr, :] = slope

        mine = dst.at[pl.ds(pl.multiple_of(row0, 16), rows), :]
        st[i, "n1"] = send(mine, mine, zup)
        st[i, "n2"] = send(mine, mine, zdn)

    def s3(i):
        b, _, rows, off = shape(i)
        dst = G if ITEMS[i][0] else H
        up = pl.ds(pl.multiple_of(b * CH + lax.rem(z + 3, 4) * QT + off, 16), rows)
        dn = pl.ds(pl.multiple_of(b * CH + lax.rem(z + 1, 4) * QT + off, 16), rows)
        st[i, "n1"].wait_recv()
        st[i, "w1"] = send(dst.at[up, AL], dst.at[up, AL], zup)
        st[i, "n2"].wait_recv()
        st[i, "w2"] = send(dst.at[dn, AR], dst.at[dn, AR], zdn)

    def flip(src, dst, b, width):
        @pl.loop(0, width // 128)
        def _(n):
            c = pl.ds(pl.multiple_of(n * 128, 128), 128)
            dst[c, pl.ds(b * CH, CH)] = src[pl.ds(b * CH, CH), c].T

    def s4(i):
        q, _, part, _ = ITEMS[i]
        b, _, rows, off = shape(i)
        st[i, "w1"].wait_recv()
        st[i, "w2"].wait_recv()
        if not q:
            if part != 0:
                flip(H, HT, b, HID)
            return
        cs = CS.at[b]
        mine = pl.ds(off * 2, 2 * rows)

        @pl.loop(0, 6)
        def _(n):
            cols = pl.ds(mul(n), 256)
            r = lax.dot_general(tokens(G, i), WI[cols, :], NT, preferred_element_type=F32)
            Q32[i % 2, mine, cols] = r[0 : 2 * rows]
            cs[mine, cols] = r[2 * rows : 4 * rows].astype(BF16)

        st[i, "m"] = send(cs.at[mine, :], CR.at[b, mine, :], mate)

    def s5(i):
        part = ITEMS[i][2]
        b = ITEMS[i][1]
        st[i, "m"].wait_recv()

        def add(a):
            @pl.loop(0, OWN // 16)
            def _(j):
                o = pl.multiple_of(j * 16, 16)
                rr = pl.ds(pl.multiple_of((POS[a] if part is None else a) * OWN + o, 16), 16)
                v = Q32[i % 2, rr, :] + CR[b, rr, :].astype(F32)
                if a:
                    QS[b, a - 1, pl.ds(o, 16), :] = v.astype(BF16)
                else:
                    QO[b, pl.ds(o, 16), :] = v

        for a in (2, 1, 3, 0) if part is None else ((2, 3) if part else (1, 0)):
            add(a)
            if a:
                st["q", b, a] = send(QS.at[b, a - 1], RA.at[b, a - 1], first(4 - a))

    def s6(i):
        b = ITEMS[i][1]
        for a in (1, 3, 2):
            st["q", b, a].wait_recv()
        if b == 0:
            for k in range(3):
                st["x", k].wait_recv()

        @pl.loop(0, OWN // 16)
        def _(j):
            rr = pl.ds(pl.multiple_of(j * 16, 16), 16)
            v = QO[b, rr, :] + RA[b, 0, rr, :].astype(F32) + RA[b, 1, rr, :].astype(F32) + RA[b, 2, rr, :].astype(F32)
            if b:
                QB[b - 1, rr, :] = v.astype(BF16)
            else:
                IG[rr, :] = (
                    v + RB[0, rr, :].astype(F32) + RB[1, rr, :].astype(F32) + RB[2, rr, :].astype(F32)
                )

        if b:
            st["x", b - 1] = send(QB.at[b - 1], RB.at[b - 1], second(4 - b))

    outs = {}

    def put(k, dst):
        c = pltpu.make_async_copy(OUT.at[k % 2], dst, osem.at[k])
        c.start()
        outs[k] = c

    def w_out_away():
        @pl.loop(0, 6)
        def _(t):
            m, n = lax.div(t, 3), lax.rem(t, 3)
            rows = pl.ds(pl.multiple_of(m * 384, 384), 384)
            cols = pl.ds(pl.multiple_of((1 - d) * HID + n * 256, 256), 256)
            r = lax.dot_general(HT[rows, :], S[:, cols], NN, preferred_element_type=F32)
            WS[rows, pl.ds(mul(n), 256)] = r.astype(BF16)

        for k in range(2):
            rows, down = pl.ds(k * 192, 192), pl.ds(384 + k * 192, 192)
            st["s1", k] = send(WS.at[rows, :], WRU.at[rows, :], xup)
            st["s2", k] = send(WS.at[down, :], WRD.at[rows, :], xdn)

    def w_out_home(m):
        @pl.loop(0, 3)
        def _(n):
            cols = pl.ds(pl.multiple_of(d * HID + n * 256, 256), 256)
            r = lax.dot_general(HT[pl.ds(m * 384, 384), :], S[:, cols], NN, preferred_element_type=F32)
            OUT[m, :, pl.ds(mul(n), 256)] = r

        put(m, woutg_hbm.at[pl.ds(pl.multiple_of(d * HID + m * 384, 384), 384), :])

    def relay_swap(k):
        rows, down = pl.ds(k * 192, 192), pl.ds(384 + k * 192, 192)
        st["s1", k].wait_recv()
        st["t", 0, k] = send(WRU.at[rows, :], WR.at[rows, :], xup)
        st["s2", k].wait_recv()
        st["t", 1, k] = send(WRD.at[rows, :], WR.at[down, :], xdn)

    def w_out_far(m):
        for k in range(2):
            st["t", m, k].wait_recv()
        outs[m].wait()

        @pl.loop(0, 12)
        def _(j):
            o = pl.multiple_of(j * 32, 32)
            OUT[m, pl.ds(o, 32), :] = WR[pl.ds(pl.multiple_of(m * 384 + o, 32), 32), :].astype(F32)

        put(2 + m, woutg_hbm.at[pl.ds(pl.multiple_of((1 - d) * HID + m * 384, 384), 384), :])

    def w_in_most(m):
        rows = pl.ds(m * 384, 384)

        @pl.loop(0, 3)
        def _(n):
            cols = pl.ds(mul(n), 256)
            WG[rows, cols] = lax.dot_general(
                XT[rows, pl.ds(CH, 3 * CH)], G[pl.ds(CH, 3 * CH), cols], NN, preferred_element_type=F32
            )

    def w_in_rest(m):
        rows = pl.ds(m * 384, 384)

        @pl.loop(0, 3)
        def _(n):
            cols = pl.ds(mul(n), 256)
            WG[rows, cols] += lax.dot_general(
                XT[rows, pl.ds(0, CH)], G[pl.ds(0, CH), cols], NN, preferred_element_type=F32
            )

        outs[4 + m] = pltpu.make_async_copy(WG.at[rows, :], wing_hbm.at[rows, :], osem.at[4 + m])
        outs[4 + m].start()

    ld_x.wait()
    gx.begin()
    ld_g.wait()
    key = mix_bits(mix_bits(step_ref[0] + jnp.int32(1013904223)) ^ seed_ref[0])
    row0 = (d * 16 + col) * OWN

    @pl.loop(0, OWN // 16)
    def _(j):
        rr = pl.ds(pl.multiple_of(j * 16, 16), 16)
        rows = lax.broadcasted_iota(I32, (16, FEAT), 0) + (row0 + j * 16)
        cols = lax.broadcasted_iota(I32, (16, FEAT), 1) + z * FEAT
        hashed = mix_bits((rows * jnp.int32(D) + cols) ^ key)
        keep = (hashed & jnp.int32(16777215)) < jnp.int32(15099494)
        v = jnp.where(keep, OG[rr, :].astype(F32) * keep_scale, jnp.zeros((), F32))
        S[rr, :] = v.astype(BF16)

    gx.firsts()
    ld_wi.wait()
    s0(0)
    gx.firsts_two()
    s0(1)
    s1(0)
    gx.seconds(0)
    gx.seconds(1)
    gx.seconds(3)
    s1(1)
    s2(0)
    gx.seconds(2)
    s2(1)
    s0(2)
    s3(0)
    s3(1)
    s1(2)
    gx.thirds()
    gs.begin()
    s0(3)
    s2(2)
    s4(0)
    s4(1)
    s1(3)
    gs.firsts()
    s3(2)
    gs.firsts_two()
    s0(4)
    s2(3)
    s4(2)
    s1(4)
    gs.seconds(0)
    gs.seconds(1)
    s3(3)
    gs.seconds(3)
    gs.seconds(2)
    ld_wo.wait()
    s0(5)
    s2(4)
    s4(3)
    s1(5)
    gs.thirds()
    flip(X, XT, 0, FEAT)
    s3(4)
    s0(6)
    s2(5)
    flip(X, XT, 1, FEAT)
    s4(4)
    s1(6)
    gs.ready(0)
    gs.ready(3)
    w_out_away()
    s3(5)
    s0(7)
    s2(6)
    s4(5)
    s1(7)
    w_out_home(0)
    relay_swap(0)
    s3(6)
    s0(8)
    s2(7)
    s5(5)
    flip(X, XT, 2, FEAT)
    s1(8)
    relay_swap(1)
    s0(9)
    s4(6)
    s3(7)
    s2(8)
    s1(9)
    flip(X, XT, 3, FEAT)
    s3(8)
    s5(6)
    s6(5)
    s2(9)
    s4(7)
    w_in_most(0)
    s3(9)
    s5(7)
    s4(8)
    w_in_most(1)
    s4(9)
    s6(6)
    w_in_most(2)
    s5(8)
    s5(9)
    s6(7)
    w_out_home(1)
    w_in_rest(0)
    w_in_rest(1)
    w_in_rest(2)
    w_in_most(3)
    w_in_rest(3)
    s6(9)
    w_out_far(0)
    w_out_far(1)
    fin = pltpu.make_async_copy(IG, ig_hbm, osem.at[8])
    fin.start()
    fin.wait()
    for m in range(2, 8):
        outs[m].wait()
    for copy in started:
        copy.wait_send()


def per_device(layer_input, w_in, w_out, out_grad, drop_seed, drop_step):
    hbm = pl.BlockSpec(memory_space=pl.ANY)
    smem = pl.BlockSpec(memory_space=pltpu.SMEM)

    def b(*shape):
        return pltpu.VMEM(shape, BF16)

    def f(*shape):
        return pltpu.VMEM(shape, F32)

    return pl.pallas_call(
        kernel,
        out_shape=(
            jax.ShapeDtypeStruct((OWN, FEAT), F32),
            jax.ShapeDtypeStruct((FEAT, HID), F32),
            jax.ShapeDtypeStruct((2 * HID, HID), F32),
        ),
        in_specs=[hbm, hbm, hbm, hbm, smem, smem],
        out_specs=(hbm, hbm, hbm),
        scratch_shapes=[
            b(1536, FEAT), b(1536, FEAT), b(FEAT, 1536), b(HID, 1536), b(1536, HID), b(1536, HID),
            b(FEAT, HID), b(HID, FEAT), b(OWN, FEAT),
            f(2, CH, HID), b(8, CH, HID), b(8, QT, 384), b(8, QT, 384), b(8, QT, 384), b(8, QT, 384),
            b(8, QT, HID), b(8, QT, HID), f(4, QT, HID),
            f(2, 192, FEAT), f(4, OWN, FEAT), b(4, 192, FEAT), b(4, 192, FEAT), b(4, 3, OWN, FEAT),
            b(4, 3, OWN, FEAT), b(3, OWN, FEAT), b(3, OWN, FEAT), f(OWN, FEAT),
            b(HID, HID), b(384, HID), b(384, HID), b(HID, HID), f(2, 384, HID), f(FEAT, HID),
            pltpu.SemaphoreType.DMA((N_SEMS,)),
            pltpu.SemaphoreType.DMA((4,)),
            pltpu.SemaphoreType.DMA((9,)),
        ],
        compiler_params=pltpu.CompilerParams(
            collective_id=0, has_side_effects=True, vmem_limit_bytes=67_000_000
        ),
        name="mlp_backward",
    )(layer_input, w_in, w_out, out_grad, drop_seed, drop_step)


def solution(mesh):
    placed = (
        P(("depth", "col"), "row"),
        P("row", "col"),
        P("col", "row"),
        P(("depth", "col"), "row"),
        P(),
        P(),
    )
    return jax.shard_map(
        per_device,
        mesh=mesh,
        in_specs=placed,
        out_specs=(
            P(("depth", "col"), "row"),
            P("row", ("col", "depth")),
            P("col", ("row", "depth")),
        ),
        check_vma=False,
    )
```

```python
import math

import jax
import jax.numpy as jnp
from jax import lax
from jax.experimental import pallas as pl
from jax.experimental.pallas import tpu as pltpu
from jax.sharding import PartitionSpec as P

D = 6144
keep_scale = 1.0 / 0.9
gelu_coef = math.sqrt(2.0 / math.pi)
F32, BF16, I32 = jnp.float32, jnp.bfloat16, jnp.int32
MESH = pl.DeviceIdType.MESH

OWN = 48
CH = 384
QT = 96
HID = 768
FEAT = 1536
ITEMS = [
    (0, 0, 0, 0), (0, 0, 1, 0), (0, 1, None, 1), (0, 3, None, 2), (0, 2, None, 3),
    (1, 1, None, 4), (1, 2, None, 5), (1, 3, None, 6), (1, 0, 1, 7), (1, 0, 0, 7),
]
POS = (0, 2, 1, 3)
N_SEMS = 400

NN = (((1,), (0,)), ((), ()))
NT = (((1,), (1,)), ((), ()))


def mix_bits(v):
    v = v ^ lax.shift_right_logical(v, jnp.int32(16))
    v = v * jnp.int32(2146121005)
    v = v ^ lax.shift_right_logical(v, jnp.int32(15))
    v = v * jnp.int32(-2073254261)
    v = v ^ lax.shift_right_logical(v, jnp.int32(16))
    return v


def gelu_parts(h):
    inner_arg = gelu_coef * (h + 0.044715 * h * h * h)
    t = jnp.tanh(inner_arg)
    act = 0.5 * h * (1.0 + t)
    slope = 0.5 * (1.0 + t) + 0.5 * h * (1.0 - t * t) * gelu_coef * (1.0 + 3.0 * 0.044715 * h * h)
    return act, slope


def slot(b, region, a):
    return pl.ds(((b * 2 + region) * 4 + POS[a]) * OWN, OWN)


def kernel(
    x_hbm, win_hbm, wout_hbm, og_hbm, seed_ref, step_ref,
    IG, WG, WOG,
    X, S, XT, HT, H, G, WI, WO, OG,
    PF, PB, RU, RD, C1, C2, FB, FA, SL,
    Q32, QO, CS, CR, QS, RA, QB, RB,
    WS, WRU, WRD, WR,
    sems, lsem,
):
    z = lax.axis_index("row")
    col = lax.axis_index("col")
    d = lax.axis_index("depth")
    core = lax.rem(col, 2)
    x = d * 2 + lax.rem(lax.div(col, 2), 2)
    y = lax.div(col, 4)

    def dev(xx, yy, zz, cc):
        xx, yy, zz = lax.rem(xx, 4), lax.rem(yy, 4), lax.rem(zz, 4)
        return {"row": zz, "col": yy * 4 + lax.rem(xx, 2) * 2 + cc, "depth": lax.div(xx, 2)}

    def first(k):
        return dev(x + k * (1 - core), y + k * core, z, core)

    def second(k):
        return dev(x + k * core, y + k * (1 - core), z, core)

    zup, zdn = dev(x, y, z + 1, core), dev(x, y, z + 3, core)
    xup, xdn = dev(x + 1, y, z, core), dev(x + 3, y, z, core)
    mate = dev(x, y, z, 1 - core)

    started = []

    def send(src, dst, to):
        k = 2 * len(started)
        copy = pltpu.make_async_remote_copy(
            src_ref=src, dst_ref=dst, send_sem=sems.at[k], recv_sem=sems.at[k + 1],
            device_id=to, device_id_type=MESH,
        )
        copy.start()
        started.append(copy)
        return copy

    def load(src, dst, k):
        c = pltpu.make_async_copy(src, dst, lsem.at[k])
        c.start()
        return c

    own = slot(0, 0, 0)
    half = pl.ds(pl.multiple_of(d * HID, HID), HID)
    other = pl.ds(pl.multiple_of((1 - d) * HID, HID), HID)
    ld_x = load(x_hbm, X.at[own, :], 0)
    ld_g = load(og_hbm, OG, 1)
    ld_wi = load(win_hbm.at[:, half], WI, 2)
    ld_wo = load(wout_hbm.at[half, :], WO, 3)

    barrier = pltpu.get_barrier_semaphore()
    near = [first(1), first(3), first(2), second(1), second(3), second(2), zup, zdn, mate]
    for n in near:
        pl.semaphore_signal(barrier, inc=1, device_id=n, device_id_type=MESH)
    pl.semaphore_wait(barrier, len(near))

    LH, RH = pl.ds(0, 768), pl.ds(768, 768)

    class Gather:
        def __init__(self, buf):
            self.buf = buf
            self.c = {}

        def spread(self, a):
            sl = self.buf.at[slot(0, 0, a), :]
            self.c[a, 1] = send(sl, self.buf.at[slot(1, 0, a), :], second(1))
            self.c[a, 3] = send(sl, self.buf.at[slot(3, 0, a), :], second(3))

        def share(self, a, b):
            self.c["m", a, b] = send(self.buf.at[slot(b, 0, a), :], self.buf.at[slot(b, 1, a), :], mate)

        def begin(self):
            sl = self.buf.at[own, :]
            self.f1 = send(sl, self.buf.at[slot(0, 0, 1), :], first(1))
            self.f3 = send(sl, self.buf.at[slot(0, 0, 3), :], first(3))
            self.share(0, 0)

        def firsts(self):
            self.f1.wait_recv()
            l = send(self.buf.at[slot(0, 0, 1), LH], self.buf.at[slot(0, 0, 2), LH], first(1))
            self.share(1, 0)
            self.f3.wait_recv()
            r = send(self.buf.at[slot(0, 0, 3), RH], self.buf.at[slot(0, 0, 2), RH], first(3))
            self.share(3, 0)
            for a in (0, 1, 3):
                self.spread(a)
            self.l, self.r = l, r

        def firsts_two(self):
            self.l.wait_recv()
            self.r.wait_recv()
            self.share(2, 0)
            self.spread(2)

        def seconds(self, a):
            self.c[a, 1].wait_recv()
            self.c[a, "l"] = send(self.buf.at[slot(1, 0, a), LH], self.buf.at[slot(2, 0, a), LH], second(1))
            self.share(a, 1)
            self.c[a, 3].wait_recv()
            self.c[a, "r"] = send(self.buf.at[slot(3, 0, a), RH], self.buf.at[slot(2, 0, a), RH], second(3))
            self.share(a, 3)

        def thirds(self):
            for a in (0, 1, 3, 2):
                self.c[a, "l"].wait_recv()
                self.c[a, "r"].wait_recv()
                self.share(a, 2)

        def ready(self, b, slots=(0, 1, 3, 2)):
            for a in slots:
                shared = self.c.pop(("m", a, b), None)
                if shared is not None:
                    shared.wait_recv()

    gx, gs = Gather(X), Gather(S)

    def mul(n):
        return pl.multiple_of(n * 256, 256)

    st = {}
    AL, AR = pl.ds(0, 384), pl.ds(384, 384)

    def shape(i):
        _, b, part, k = ITEMS[i]
        rows = QT if part is None else OWN
        return b, k, rows, (part or 0) * OWN

    def quarter(k, rows):
        return pl.multiple_of(lax.rem(z + k, 4) * rows, 16)

    def tokens(buf, i, cols=None):
        b, _, rows, off = shape(i)
        if rows == QT:
            return buf[pl.ds(b * CH, CH), :]
        return jnp.concatenate([buf[pl.ds(b * CH + g * QT + off, OWN), :] for g in range(4)], axis=0)

    def s0(i):
        q = ITEMS[i][0]
        b, k, rows, off = shape(i)
        base = off * 4
        pf, pb = PF.at[i % 2], PB.at[k]
        (gs if q else gx).ready(b, (0, 1, 3, 2) if rows == QT else ((2, 3) if off else (0, 1)))

        @pl.loop(0, 3)
        def _(n):
            cols = pl.ds(mul(n), 256)
            if q:
                r = lax.dot_general(tokens(S, i), WO[cols, :], NT, preferred_element_type=F32)
            else:
                r = lax.dot_general(tokens(X, i), WI[:, cols], NN, preferred_element_type=F32)
            pf[pl.ds(0, 4 * rows), cols] = r
            pb[pl.ds(base, 4 * rows), cols] = r.astype(BF16)

        def part(j):
            return pl.ds(base + quarter(j, rows), rows)

        mine = pl.ds(off, rows)
        st[i, "a1"] = send(pb.at[part(2), AL], RU.at[k, mine], zup)
        st[i, "a2"] = send(pb.at[part(2), AR], RD.at[k, mine], zdn)
        st[i, "b1"] = send(pb.at[part(1), AR], FB.at[k, mine, AR], zup)
        st[i, "b2"] = send(pb.at[part(3), AL], FA.at[k, mine, AL], zdn)

    def s1(i):
        _, k, rows, off = shape(i)
        pf = PF.at[i % 2]
        mine = pl.ds(off, rows)

        def add(relay, out, j, cols):
            base = quarter(j, rows)

            @pl.loop(0, rows // 16)
            def _(t):
                o = pl.multiple_of(t * 16, 16)
                rr = pl.ds(off + o, 16)
                src = pl.ds(pl.multiple_of(base + o, 16), 16)
                out[rr, :] = (relay[rr, :].astype(F32) + pf[src, cols]).astype(BF16)

        st[i, "a1"].wait_recv()
        add(RU.at[k], C1.at[k], 1, AL)
        st[i, "c1"] = send(C1.at[k, mine], FB.at[k, mine, AL], zup)
        st[i, "a2"].wait_recv()
        add(RD.at[k], C2.at[k], 3, AR)
        st[i, "c2"] = send(C2.at[k, mine], FA.at[k, mine, AR], zdn)

    def s2(i):
        q = ITEMS[i][0]
        b, k, rows, off = shape(i)
        pf = PF.at[i % 2]
        for key in ("b1", "b2", "c1", "c2"):
            st[i, key].wait_recv()
        dst = G if q else H
        row0 = b * CH + z * QT + off
        base = quarter(0, rows)

        @pl.loop(0, rows // 16)
        def _(t):
            o = pl.multiple_of(t * 16, 16)
            rr = pl.ds(off + o, 16)
            src = pl.ds(pl.multiple_of(base + o, 16), 16)
            to = pl.ds(pl.multiple_of(row0 + o, 16), 16)
            v = pf[src, :] + FB[k, rr, :].astype(F32) + FA[k, rr, :].astype(F32)
            if q:
                dst[to, :] = (v * SL[b, rr, :]).astype(BF16)
            else:
                act, slope = gelu_parts(v)
                dst[to, :] = act.astype(BF16)
                SL[b, rr, :] = slope

        mine = dst.at[pl.ds(pl.multiple_of(row0, 16), rows), :]
        st[i, "n1"] = send(mine, mine, zup)
        st[i, "n2"] = send(mine, mine, zdn)

    def s3(i):
        b, _, rows, off = shape(i)
        dst = G if ITEMS[i][0] else H
        up = pl.ds(pl.multiple_of(b * CH + lax.rem(z + 3, 4) * QT + off, 16), rows)
        dn = pl.ds(pl.multiple_of(b * CH + lax.rem(z + 1, 4) * QT + off, 16), rows)
        st[i, "n1"].wait_recv()
        st[i, "w1"] = send(dst.at[up, AL], dst.at[up, AL], zup)
        st[i, "n2"].wait_recv()
        st[i, "w2"] = send(dst.at[dn, AR], dst.at[dn, AR], zdn)

    def flip(src, dst, b, width):
        @pl.loop(0, width // 128)
        def _(n):
            c = pl.ds(pl.multiple_of(n * 128, 128), 128)
            dst[c, pl.ds(b * CH, CH)] = src[pl.ds(b * CH, CH), c].T

    def s4(i):
        q, _, part, _ = ITEMS[i]
        b, _, rows, off = shape(i)
        st[i, "w1"].wait_recv()
        st[i, "w2"].wait_recv()
        if not q:
            if part != 0:
                flip(H, HT, b, HID)
            return
        cs = CS.at[b]
        mine = pl.ds(off * 2, 2 * rows)

        @pl.loop(0, 6)
        def _(n):
            cols = pl.ds(mul(n), 256)
            r = lax.dot_general(tokens(G, i), WI[cols, :], NT, preferred_element_type=F32)
            Q32[i % 2, mine, cols] = r[0 : 2 * rows]
            cs[mine, cols] = r[2 * rows : 4 * rows].astype(BF16)

        st[i, "m"] = send(cs.at[mine, :], CR.at[b, mine, :], mate)

    def s5(i):
        part = ITEMS[i][2]
        b = ITEMS[i][1]
        st[i, "m"].wait_recv()

        def add(a):
            @pl.loop(0, OWN // 16)
            def _(j):
                o = pl.multiple_of(j * 16, 16)
                rr = pl.ds(pl.multiple_of((POS[a] if part is None else a) * OWN + o, 16), 16)
                v = Q32[i % 2, rr, :] + CR[b, rr, :].astype(F32)
                if a:
                    QS[b, a - 1, pl.ds(o, 16), :] = v.astype(BF16)
                else:
                    QO[b, pl.ds(o, 16), :] = v

        for a in (2, 1, 3, 0) if part is None else ((2, 3) if part else (1, 0)):
            add(a)
            if a:
                st["q", b, a] = send(QS.at[b, a - 1], RA.at[b, a - 1], first(4 - a))

    def s6(i):
        b = ITEMS[i][1]
        for a in (1, 3, 2):
            st["q", b, a].wait_recv()
        if b == 0:
            for k in range(3):
                st["x", k].wait_recv()

        @pl.loop(0, OWN // 16)
        def _(j):
            rr = pl.ds(pl.multiple_of(j * 16, 16), 16)
            v = QO[b, rr, :] + RA[b, 0, rr, :].astype(F32) + RA[b, 1, rr, :].astype(F32) + RA[b, 2, rr, :].astype(F32)
            if b:
                QB[b - 1, rr, :] = v.astype(BF16)
            else:
                IG[rr, :] = (
                    v + RB[0, rr, :].astype(F32) + RB[1, rr, :].astype(F32) + RB[2, rr, :].astype(F32)
                )

        if b:
            st["x", b - 1] = send(QB.at[b - 1], RB.at[b - 1], second(4 - b))

    def w_out_away():
        @pl.loop(0, 6)
        def _(t):
            m, n = lax.div(t, 3), lax.rem(t, 3)
            rows = pl.ds(pl.multiple_of(m * 384, 384), 384)
            cols = pl.ds(pl.multiple_of((1 - d) * HID + n * 256, 256), 256)
            r = lax.dot_general(HT[rows, :], S[:, cols], NN, preferred_element_type=F32)
            WS[rows, pl.ds(mul(n), 256)] = r.astype(BF16)

        for k in range(2):
            rows, down = pl.ds(k * 192, 192), pl.ds(384 + k * 192, 192)
            st["s1", k] = send(WS.at[rows, :], WRU.at[rows, :], xup)
            st["s2", k] = send(WS.at[down, :], WRD.at[rows, :], xdn)

    def w_out_home(m):
        @pl.loop(0, 3)
        def _(n):
            cols = pl.ds(pl.multiple_of(d * HID + n * 256, 256), 256)
            r = lax.dot_general(HT[pl.ds(m * 384, 384), :], S[:, cols], NN, preferred_element_type=F32)
            WOG[pl.ds(pl.multiple_of(d * HID + m * 384, 384), 384), pl.ds(mul(n), 256)] = r

    def relay_swap(k):
        rows, down = pl.ds(k * 192, 192), pl.ds(384 + k * 192, 192)
        st["s1", k].wait_recv()
        st["t", 0, k] = send(WRU.at[rows, :], WR.at[rows, :], xup)
        st["s2", k].wait_recv()
        st["t", 1, k] = send(WRD.at[rows, :], WR.at[down, :], xdn)

    def w_out_far(m):
        for k in range(2):
            st["t", m, k].wait_recv()

        @pl.loop(0, 12)
        def _(j):
            o = pl.multiple_of(j * 32, 32)
            to = pl.ds(pl.multiple_of((1 - d) * HID + m * 384 + o, 32), 32)
            WOG[to, :] = WR[pl.ds(pl.multiple_of(m * 384 + o, 32), 32), :].astype(F32)

    def w_in_most(m):
        rows = pl.ds(m * 384, 384)

        @pl.loop(0, 3)
        def _(n):
            cols = pl.ds(mul(n), 256)
            WG[rows, cols] = lax.dot_general(
                XT[rows, pl.ds(CH, 3 * CH)], G[pl.ds(CH, 3 * CH), cols], NN, preferred_element_type=F32
            )

    def w_in_rest(m):
        rows = pl.ds(m * 384, 384)

        @pl.loop(0, 3)
        def _(n):
            cols = pl.ds(mul(n), 256)
            WG[rows, cols] += lax.dot_general(
                XT[rows, pl.ds(0, CH)], G[pl.ds(0, CH), cols], NN, preferred_element_type=F32
            )

    ld_x.wait()
    gx.begin()
    ld_g.wait()
    key = mix_bits(mix_bits(step_ref[0] + jnp.int32(1013904223)) ^ seed_ref[0])
    row0 = (d * 16 + col) * OWN

    @pl.loop(0, OWN // 16)
    def _(j):
        rr = pl.ds(pl.multiple_of(j * 16, 16), 16)
        rows = lax.broadcasted_iota(I32, (16, FEAT), 0) + (row0 + j * 16)
        cols = lax.broadcasted_iota(I32, (16, FEAT), 1) + z * FEAT
        hashed = mix_bits((rows * jnp.int32(D) + cols) ^ key)
        keep = (hashed & jnp.int32(16777215)) < jnp.int32(15099494)
        v = jnp.where(keep, OG[rr, :].astype(F32) * keep_scale, jnp.zeros((), F32))
        S[rr, :] = v.astype(BF16)

    gx.firsts()
    ld_wi.wait()
    s0(0)
    gx.firsts_two()
    s0(1)
    s1(0)
    gx.seconds(0)
    gx.seconds(1)
    gx.seconds(3)
    s1(1)
    s2(0)
    gx.seconds(2)
    s2(1)
    s0(2)
    s3(0)
    s3(1)
    s1(2)
    gx.thirds()
    gs.begin()
    s0(3)
    s2(2)
    s4(0)
    s4(1)
    s1(3)
    gs.firsts()
    s3(2)
    gs.firsts_two()
    s0(4)
    s2(3)
    s4(2)
    s1(4)
    gs.seconds(0)
    gs.seconds(1)
    s3(3)
    gs.seconds(3)
    gs.seconds(2)
    ld_wo.wait()
    s0(5)
    s2(4)
    s4(3)
    s1(5)
    gs.thirds()
    flip(X, XT, 0, FEAT)
    s3(4)
    s0(6)
    s2(5)
    flip(X, XT, 1, FEAT)
    s4(4)
    s1(6)
    gs.ready(0)
    gs.ready(3)
    w_out_away()
    s3(5)
    s0(7)
    s2(6)
    s4(5)
    s1(7)
    w_out_home(0)
    relay_swap(0)
    s3(6)
    s0(8)
    s2(7)
    s5(5)
    flip(X, XT, 2, FEAT)
    s1(8)
    relay_swap(1)
    s0(9)
    s4(6)
    s3(7)
    s2(8)
    s1(9)
    flip(X, XT, 3, FEAT)
    s3(8)
    s5(6)
    s6(5)
    s2(9)
    s4(7)
    w_in_most(0)
    s3(9)
    s5(7)
    s4(8)
    w_in_most(1)
    s4(9)
    s6(6)
    w_in_most(2)
    s5(8)
    s5(9)
    s6(7)
    w_out_home(1)
    w_in_rest(0)
    w_in_rest(1)
    w_in_rest(2)
    w_in_most(3)
    w_in_rest(3)
    s6(9)
    w_out_far(0)
    w_out_far(1)
    for copy in started:
        copy.wait_send()


def per_device(layer_input, w_in, w_out, out_grad, drop_seed, drop_step):
    hbm = pl.BlockSpec(memory_space=pl.ANY)
    smem = pl.BlockSpec(memory_space=pltpu.SMEM)

    def b(*shape):
        return pltpu.VMEM(shape, BF16)

    def f(*shape):
        return pltpu.VMEM(shape, F32)

    return pl.pallas_call(
        kernel,
        out_shape=(
            pltpu.VMEM((OWN, FEAT), F32),
            pltpu.VMEM((FEAT, HID), F32),
            pltpu.VMEM((2 * HID, HID), F32),
        ),
        in_specs=[hbm, hbm, hbm, hbm, smem, smem],
        out_specs=(pl.BlockSpec(memory_space=pltpu.VMEM),) * 3,
        scratch_shapes=[
            b(1536, FEAT), b(1536, FEAT), b(FEAT, 1536), b(HID, 1536), b(1536, HID), b(1536, HID),
            b(FEAT, HID), b(HID, FEAT), b(OWN, FEAT),
            f(2, CH, HID), b(8, CH, HID), b(8, QT, 384), b(8, QT, 384), b(8, QT, 384), b(8, QT, 384),
            b(8, QT, HID), b(8, QT, HID), f(4, QT, HID),
            f(2, 192, FEAT), f(4, OWN, FEAT), b(4, 192, FEAT), b(4, 192, FEAT), b(4, 3, OWN, FEAT),
            b(4, 3, OWN, FEAT), b(3, OWN, FEAT), b(3, OWN, FEAT),
            b(HID, HID), b(384, HID), b(384, HID), b(HID, HID),
            pltpu.SemaphoreType.DMA((N_SEMS,)),
            pltpu.SemaphoreType.DMA((4,)),
        ],
        compiler_params=pltpu.CompilerParams(
            collective_id=0, has_side_effects=True, vmem_limit_bytes=56_500_000
        ),
        name="mlp_backward",
    )(layer_input, w_in, w_out, out_grad, drop_seed, drop_step)


def solution(mesh):
    placed = (
        P(("depth", "col"), "row"),
        P("row", "col"),
        P("col", "row"),
        P(("depth", "col"), "row"),
        P(),
        P(),
    )
    return jax.shard_map(
        per_device,
        mesh=mesh,
        in_specs=placed,
        out_specs=(
            P(("depth", "col"), "row"),
            P("row", ("col", "depth")),
            P("col", ("row", "depth")),
        ),
        check_vma=False,
    )
```

```python
import math

import jax
import jax.numpy as jnp
from jax import lax
from jax.experimental import pallas as pl
from jax.experimental.pallas import tpu as pltpu
from jax.sharding import PartitionSpec as P

D = 6144
keep_scale = 1.0 / 0.9
gelu_coef = math.sqrt(2.0 / math.pi)
F32, BF16, I32 = jnp.float32, jnp.bfloat16, jnp.int32
MESH = pl.DeviceIdType.MESH

OWN = 48
CH = 384
QT = 96
HID = 768
FEAT = 1536
ITEMS = [
    (0, 0, 0, 0), (0, 0, 1, 0), (0, 1, None, 1), (0, 3, None, 2), (0, 2, None, 3),
    (1, 1, None, 4), (1, 2, None, 5), (1, 3, None, 6), (1, 0, 1, 7), (1, 0, 0, 7),
]
POS = (0, 2, 1, 3)
N_SEMS = 400

NN = (((1,), (0,)), ((), ()))
NT = (((1,), (1,)), ((), ()))


def mix_bits(v):
    v = v ^ lax.shift_right_logical(v, jnp.int32(16))
    v = v * jnp.int32(2146121005)
    v = v ^ lax.shift_right_logical(v, jnp.int32(15))
    v = v * jnp.int32(-2073254261)
    v = v ^ lax.shift_right_logical(v, jnp.int32(16))
    return v


def gelu_parts(h):
    inner_arg = gelu_coef * (h + 0.044715 * h * h * h)
    t = jnp.tanh(inner_arg)
    act = 0.5 * h * (1.0 + t)
    slope = 0.5 * (1.0 + t) + 0.5 * h * (1.0 - t * t) * gelu_coef * (1.0 + 3.0 * 0.044715 * h * h)
    return act, slope


def slot(b, region, a):
    return pl.ds(((b * 2 + region) * 4 + POS[a]) * OWN, OWN)


def kernel(
    x_hbm, win_hbm, wout_hbm, og_hbm, seed_ref, step_ref,
    IG, WG, WOG,
    X, S, XT, HT, H, G, WI, WO, OG,
    PF, PB, RU, RD, C1, C2, FB, FA, SL,
    Q32, QO, CS, CR, QS, RA, QB, RB,
    WS, WRU, WRD, WR,
    sems, lsem,
):
    z = lax.axis_index("row")
    col = lax.axis_index("col")
    d = lax.axis_index("depth")
    core = lax.rem(col, 2)
    x = d * 2 + lax.rem(lax.div(col, 2), 2)
    y = lax.div(col, 4)

    def dev(xx, yy, zz, cc):
        xx, yy, zz = lax.rem(xx, 4), lax.rem(yy, 4), lax.rem(zz, 4)
        return {"row": zz, "col": yy * 4 + lax.rem(xx, 2) * 2 + cc, "depth": lax.div(xx, 2)}

    def first(k):
        return dev(x + k * (1 - core), y + k * core, z, core)

    def second(k):
        return dev(x + k * core, y + k * (1 - core), z, core)

    zup, zdn = dev(x, y, z + 1, core), dev(x, y, z + 3, core)
    xup, xdn = dev(x + 1, y, z, core), dev(x + 3, y, z, core)
    mate = dev(x, y, z, 1 - core)

    started = []

    def send(src, dst, to):
        k = 2 * len(started)
        copy = pltpu.make_async_remote_copy(
            src_ref=src, dst_ref=dst, send_sem=sems.at[k], recv_sem=sems.at[k + 1],
            device_id=to, device_id_type=MESH,
        )
        copy.start()
        started.append(copy)
        return copy

    def load(src, dst, k):
        c = pltpu.make_async_copy(src, dst, lsem.at[k])
        c.start()
        return c

    own = slot(0, 0, 0)
    half = pl.ds(pl.multiple_of(d * HID, HID), HID)
    other = pl.ds(pl.multiple_of((1 - d) * HID, HID), HID)
    ld_x = load(x_hbm, X.at[own, :], 0)
    ld_g = load(og_hbm, OG, 1)
    ld_wi = load(win_hbm.at[:, half], WI, 2)
    ld_wo = load(wout_hbm.at[half, :], WO, 3)

    barrier = pltpu.get_barrier_semaphore()
    near = [first(1), first(3), first(2), second(1), second(3), second(2), zup, zdn, mate]
    for n in near:
        pl.semaphore_signal(barrier, inc=1, device_id=n, device_id_type=MESH)
    pl.semaphore_wait(barrier, len(near))

    LH, RH = pl.ds(0, 768), pl.ds(768, 768)

    class Gather:
        def __init__(self, buf):
            self.buf = buf
            self.c = {}

        def spread(self, a):
            sl = self.buf.at[slot(0, 0, a), :]
            self.c[a, 1] = send(sl, self.buf.at[slot(1, 0, a), :], second(1))
            self.c[a, 3] = send(sl, self.buf.at[slot(3, 0, a), :], second(3))

        def share(self, a, b):
            self.c["m", a, b] = send(self.buf.at[slot(b, 0, a), :], self.buf.at[slot(b, 1, a), :], mate)

        def begin(self):
            sl = self.buf.at[own, :]
            self.f1 = send(sl, self.buf.at[slot(0, 0, 1), :], first(1))
            self.f3 = send(sl, self.buf.at[slot(0, 0, 3), :], first(3))
            self.share(0, 0)

        def firsts(self):
            self.f1.wait_recv()
            l = send(self.buf.at[slot(0, 0, 1), LH], self.buf.at[slot(0, 0, 2), LH], first(1))
            self.share(1, 0)
            self.f3.wait_recv()
            r = send(self.buf.at[slot(0, 0, 3), RH], self.buf.at[slot(0, 0, 2), RH], first(3))
            self.share(3, 0)
            for a in (0, 1, 3):
                self.spread(a)
            self.l, self.r = l, r

        def firsts_two(self):
            self.l.wait_recv()
            self.r.wait_recv()
            self.share(2, 0)
            self.spread(2)

        def seconds(self, a):
            self.c[a, 1].wait_recv()
            self.c[a, "l"] = send(self.buf.at[slot(1, 0, a), LH], self.buf.at[slot(2, 0, a), LH], second(1))
            self.share(a, 1)
            self.c[a, 3].wait_recv()
            self.c[a, "r"] = send(self.buf.at[slot(3, 0, a), RH], self.buf.at[slot(2, 0, a), RH], second(3))
            self.share(a, 3)

        def thirds(self):
            for a in (0, 1, 3, 2):
                self.c[a, "l"].wait_recv()
                self.c[a, "r"].wait_recv()
                self.share(a, 2)

        def ready(self, b, slots=(0, 1, 3, 2)):
            for a in slots:
                shared = self.c.pop(("m", a, b), None)
                if shared is not None:
                    shared.wait_recv()

    gx, gs = Gather(X), Gather(S)

    def mul(n):
        return pl.multiple_of(n * 256, 256)

    st = {}
    AL, AR = pl.ds(0, 384), pl.ds(384, 384)

    def shape(i):
        _, b, part, k = ITEMS[i]
        rows = QT if part is None else OWN
        return b, k, rows, (part or 0) * OWN

    def quarter(k, rows):
        return pl.multiple_of(lax.rem(z + k, 4) * rows, 16)

    def tokens(buf, i, cols=None):
        b, _, rows, off = shape(i)
        if rows == QT:
            return buf[pl.ds(b * CH, CH), :]
        return jnp.concatenate([buf[pl.ds(b * CH + g * QT + off, OWN), :] for g in range(4)], axis=0)

    def s0(i):
        q = ITEMS[i][0]
        b, k, rows, off = shape(i)
        base = off * 4
        pf, pb = PF.at[i % 2], PB.at[k]
        (gs if q else gx).ready(b, (0, 1, 3, 2) if rows == QT else ((2, 3) if off else (0, 1)))

        @pl.loop(0, 3)
        def _(n):
            cols = pl.ds(mul(n), 256)
            if q:
                r = lax.dot_general(tokens(S, i), WO[cols, :], NT, preferred_element_type=F32)
            else:
                r = lax.dot_general(tokens(X, i), WI[:, cols], NN, preferred_element_type=F32)
            pf[pl.ds(0, 4 * rows), cols] = r
            pb[pl.ds(base, 4 * rows), cols] = r.astype(BF16)

        def part(j):
            return pl.ds(base + quarter(j, rows), rows)

        mine = pl.ds(off, rows)
        st[i, "a1"] = send(pb.at[part(2), AL], RU.at[k, mine], zup)
        st[i, "a2"] = send(pb.at[part(2), AR], RD.at[k, mine], zdn)
        st[i, "b1"] = send(pb.at[part(1), AR], FB.at[k, mine, AR], zup)
        st[i, "b2"] = send(pb.at[part(3), AL], FA.at[k, mine, AL], zdn)

    def s1(i):
        _, k, rows, off = shape(i)
        pf = PF.at[i % 2]
        mine = pl.ds(off, rows)

        def add(relay, out, j, cols):
            base = quarter(j, rows)

            @pl.loop(0, rows // 16)
            def _(t):
                o = pl.multiple_of(t * 16, 16)
                rr = pl.ds(off + o, 16)
                src = pl.ds(pl.multiple_of(base + o, 16), 16)
                out[rr, :] = (relay[rr, :].astype(F32) + pf[src, cols]).astype(BF16)

        st[i, "a1"].wait_recv()
        add(RU.at[k], C1.at[k], 1, AL)
        st[i, "c1"] = send(C1.at[k, mine], FB.at[k, mine, AL], zup)
        st[i, "a2"].wait_recv()
        add(RD.at[k], C2.at[k], 3, AR)
        st[i, "c2"] = send(C2.at[k, mine], FA.at[k, mine, AR], zdn)

    def s2(i):
        q = ITEMS[i][0]
        b, k, rows, off = shape(i)
        pf = PF.at[i % 2]
        for key in ("b1", "b2", "c1", "c2"):
            st[i, key].wait_recv()
        dst = G if q else H
        row0 = b * CH + z * QT + off
        base = quarter(0, rows)

        @pl.loop(0, rows // 16)
        def _(t):
            o = pl.multiple_of(t * 16, 16)
            rr = pl.ds(off + o, 16)
            src = pl.ds(pl.multiple_of(base + o, 16), 16)
            to = pl.ds(pl.multiple_of(row0 + o, 16), 16)
            v = pf[src, :] + FB[k, rr, :].astype(F32) + FA[k, rr, :].astype(F32)
            if q:
                dst[to, :] = (v * SL[b, rr, :]).astype(BF16)
            else:
                act, slope = gelu_parts(v)
                dst[to, :] = act.astype(BF16)
                SL[b, rr, :] = slope

        mine = dst.at[pl.ds(pl.multiple_of(row0, 16), rows), :]
        st[i, "n1"] = send(mine, mine, zup)
        st[i, "n2"] = send(mine, mine, zdn)

    def s3(i):
        b, _, rows, off = shape(i)
        dst = G if ITEMS[i][0] else H
        up = pl.ds(pl.multiple_of(b * CH + lax.rem(z + 3, 4) * QT + off, 16), rows)
        dn = pl.ds(pl.multiple_of(b * CH + lax.rem(z + 1, 4) * QT + off, 16), rows)
        st[i, "n1"].wait_recv()
        st[i, "w1"] = send(dst.at[up, AL], dst.at[up, AL], zup)
        st[i, "n2"].wait_recv()
        st[i, "w2"] = send(dst.at[dn, AR], dst.at[dn, AR], zdn)

    def flip(src, dst, b, width):
        @pl.loop(0, width // 128)
        def _(n):
            c = pl.ds(pl.multiple_of(n * 128, 128), 128)
            dst[c, pl.ds(b * CH, CH)] = src[pl.ds(b * CH, CH), c].T

    def s4(i):
        q, _, part, _ = ITEMS[i]
        b, _, rows, off = shape(i)
        st[i, "w1"].wait_recv()
        st[i, "w2"].wait_recv()
        if not q:
            if part != 0:
                flip(H, HT, b, HID)
            return
        cs = CS.at[b]
        mine = pl.ds(off * 2, 2 * rows)

        @pl.loop(0, 6)
        def _(n):
            cols = pl.ds(mul(n), 256)
            r = lax.dot_general(tokens(G, i), WI[cols, :], NT, preferred_element_type=F32)
            Q32[i % 2, mine, cols] = r[0 : 2 * rows]
            cs[mine, cols] = r[2 * rows : 4 * rows].astype(BF16)

        st[i, "m"] = send(cs.at[mine, :], CR.at[b, mine, :], mate)

    def s5(i):
        part = ITEMS[i][2]
        b = ITEMS[i][1]
        st[i, "m"].wait_recv()

        def add(a):
            @pl.loop(0, OWN // 16)
            def _(j):
                o = pl.multiple_of(j * 16, 16)
                rr = pl.ds(pl.multiple_of((POS[a] if part is None else a) * OWN + o, 16), 16)
                v = Q32[i % 2, rr, :] + CR[b, rr, :].astype(F32)
                if a:
                    QS[b, a - 1, pl.ds(o, 16), :] = v.astype(BF16)
                else:
                    QO[b, pl.ds(o, 16), :] = v

        for a in (2, 1, 3, 0) if part is None else ((2, 3) if part else (1, 0)):
            add(a)
            if a:
                st["q", b, a] = send(QS.at[b, a - 1], RA.at[b, a - 1], first(4 - a))

    def s6(i):
        b = ITEMS[i][1]
        for a in (1, 3, 2):
            st["q", b, a].wait_recv()
        if b == 0:
            for k in range(3):
                st["x", k].wait_recv()

        @pl.loop(0, OWN // 16)
        def _(j):
            rr = pl.ds(pl.multiple_of(j * 16, 16), 16)
            v = QO[b, rr, :] + RA[b, 0, rr, :].astype(F32) + RA[b, 1, rr, :].astype(F32) + RA[b, 2, rr, :].astype(F32)
            if b:
                QB[b - 1, rr, :] = v.astype(BF16)
            else:
                IG[rr, :] = (
                    v + RB[0, rr, :].astype(F32) + RB[1, rr, :].astype(F32) + RB[2, rr, :].astype(F32)
                )

        if b:
            st["x", b - 1] = send(QB.at[b - 1], RB.at[b - 1], second(4 - b))

    def w_out_away():
        @pl.loop(0, 6)
        def _(t):
            m, n = lax.div(t, 3), lax.rem(t, 3)
            rows = pl.ds(pl.multiple_of(m * 384, 384), 384)
            cols = pl.ds(pl.multiple_of((1 - d) * HID + n * 256, 256), 256)
            r = lax.dot_general(HT[rows, :], S[:, cols], NN, preferred_element_type=F32)
            WS[rows, pl.ds(mul(n), 256)] = r.astype(BF16)

        for k in range(2):
            rows, down = pl.ds(k * 192, 192), pl.ds(384 + k * 192, 192)
            st["s1", k] = send(WS.at[rows, :], WRU.at[rows, :], xup)
            st["s2", k] = send(WS.at[down, :], WRD.at[rows, :], xdn)

    def w_out_home(m):
        @pl.loop(0, 3)
        def _(n):
            cols = pl.ds(pl.multiple_of(d * HID + n * 256, 256), 256)
            r = lax.dot_general(HT[pl.ds(m * 384, 384), :], S[:, cols], NN, preferred_element_type=F32)
            WOG[pl.ds(pl.multiple_of(d * HID + m * 384, 384), 384), pl.ds(mul(n), 256)] = r

    def relay_swap(k):
        rows, down = pl.ds(k * 192, 192), pl.ds(384 + k * 192, 192)
        st["s1", k].wait_recv()
        st["t", 0, k] = send(WRU.at[rows, :], WR.at[rows, :], xup)
        st["s2", k].wait_recv()
        st["t", 1, k] = send(WRD.at[rows, :], WR.at[down, :], xdn)

    def w_out_far(m):
        for k in range(2):
            st["t", m, k].wait_recv()

        @pl.loop(0, 12)
        def _(j):
            o = pl.multiple_of(j * 32, 32)
            to = pl.ds(pl.multiple_of((1 - d) * HID + m * 384 + o, 32), 32)
            WOG[to, :] = WR[pl.ds(pl.multiple_of(m * 384 + o, 32), 32), :].astype(F32)

    def w_in_most(m):
        rows = pl.ds(m * 384, 384)

        @pl.loop(0, 3)
        def _(n):
            cols = pl.ds(mul(n), 256)
            WG[rows, cols] = lax.dot_general(
                XT[rows, pl.ds(CH, 3 * CH)], G[pl.ds(CH, 3 * CH), cols], NN, preferred_element_type=F32
            )

    def w_in_rest(m):
        rows = pl.ds(m * 384, 384)

        @pl.loop(0, 3)
        def _(n):
            cols = pl.ds(mul(n), 256)
            WG[rows, cols] += lax.dot_general(
                XT[rows, pl.ds(0, CH)], G[pl.ds(0, CH), cols], NN, preferred_element_type=F32
            )

    ld_x.wait()
    gx.begin()
    ld_g.wait()
    key = mix_bits(mix_bits(step_ref[0] + jnp.int32(1013904223)) ^ seed_ref[0])
    row0 = (d * 16 + col) * OWN

    @pl.loop(0, OWN // 16)
    def _(j):
        rr = pl.ds(pl.multiple_of(j * 16, 16), 16)
        rows = lax.broadcasted_iota(I32, (16, FEAT), 0) + (row0 + j * 16)
        cols = lax.broadcasted_iota(I32, (16, FEAT), 1) + z * FEAT
        hashed = mix_bits((rows * jnp.int32(D) + cols) ^ key)
        keep = (hashed & jnp.int32(16777215)) < jnp.int32(15099494)
        v = jnp.where(keep, OG[rr, :].astype(F32) * keep_scale, jnp.zeros((), F32))
        S[rr, :] = v.astype(BF16)

    gx.firsts()
    ld_wi.wait()
    s0(0)
    gx.firsts_two()
    s0(1)
    s1(0)
    gx.seconds(0)
    gx.seconds(1)
    gx.seconds(3)
    s1(1)
    s2(0)
    gx.seconds(2)
    s2(1)
    s0(2)
    s3(0)
    s3(1)
    s1(2)
    gx.thirds()
    gs.begin()
    s0(3)
    s2(2)
    s4(0)
    s4(1)
    s1(3)
    gs.firsts()
    s3(2)
    gs.firsts_two()
    s0(4)
    s2(3)
    s4(2)
    s1(4)
    gs.seconds(0)
    gs.seconds(1)
    s3(3)
    gs.seconds(3)
    gs.seconds(2)
    ld_wo.wait()
    s0(5)
    s2(4)
    s4(3)
    s1(5)
    gs.thirds()
    flip(X, XT, 0, FEAT)
    s3(4)
    s0(6)
    s2(5)
    flip(X, XT, 1, FEAT)
    s4(4)
    s1(6)
    gs.ready(0)
    gs.ready(3)
    w_out_away()
    s3(5)
    s0(7)
    s2(6)
    s4(5)
    s1(7)
    w_out_home(0)
    relay_swap(0)
    s3(6)
    s0(8)
    s2(7)
    s5(5)
    flip(X, XT, 2, FEAT)
    s1(8)
    relay_swap(1)
    s0(9)
    s4(6)
    s3(7)
    s2(8)
    s1(9)
    flip(X, XT, 3, FEAT)
    w_out_home(1)
    s3(8)
    s2(9)
    s5(6)
    s4(7)
    s6(5)
    w_in_most(0)
    s5(7)
    s3(9)
    s4(8)
    w_in_most(1)
    s5(8)
    s6(6)
    s4(9)
    s6(7)
    w_in_most(2)
    s5(9)
    w_in_rest(0)
    w_in_rest(1)
    w_in_rest(2)
    w_in_most(3)
    w_in_rest(3)
    w_out_far(0)
    w_out_far(1)
    s6(9)
    for copy in started:
        copy.wait_send()


def per_device(layer_input, w_in, w_out, out_grad, drop_seed, drop_step):
    hbm = pl.BlockSpec(memory_space=pl.ANY)
    smem = pl.BlockSpec(memory_space=pltpu.SMEM)

    def b(*shape):
        return pltpu.VMEM(shape, BF16)

    def f(*shape):
        return pltpu.VMEM(shape, F32)

    return pl.pallas_call(
        kernel,
        out_shape=(
            pltpu.VMEM((OWN, FEAT), F32),
            pltpu.VMEM((FEAT, HID), F32),
            pltpu.VMEM((2 * HID, HID), F32),
        ),
        in_specs=[hbm, hbm, hbm, hbm, smem, smem],
        out_specs=(pl.BlockSpec(memory_space=pltpu.VMEM),) * 3,
        scratch_shapes=[
            b(1536, FEAT), b(1536, FEAT), b(FEAT, 1536), b(HID, 1536), b(1536, HID), b(1536, HID),
            b(FEAT, HID), b(HID, FEAT), b(OWN, FEAT),
            f(2, CH, HID), b(8, CH, HID), b(8, QT, 384), b(8, QT, 384), b(8, QT, 384), b(8, QT, 384),
            b(8, QT, HID), b(8, QT, HID), f(4, QT, HID),
            f(2, 192, FEAT), f(4, OWN, FEAT), b(4, 192, FEAT), b(4, 192, FEAT), b(4, 3, OWN, FEAT),
            b(4, 3, OWN, FEAT), b(3, OWN, FEAT), b(3, OWN, FEAT),
            b(HID, HID), b(384, HID), b(384, HID), b(HID, HID),
            pltpu.SemaphoreType.DMA((N_SEMS,)),
            pltpu.SemaphoreType.DMA((4,)),
        ],
        compiler_params=pltpu.CompilerParams(
            collective_id=0, has_side_effects=True, vmem_limit_bytes=56_500_000
        ),
        name="mlp_backward",
    )(layer_input, w_in, w_out, out_grad, drop_seed, drop_step)


def solution(mesh):
    placed = (
        P(("depth", "col"), "row"),
        P("row", "col"),
        P("col", "row"),
        P(("depth", "col"), "row"),
        P(),
        P(),
    )
    return jax.shard_map(
        per_device,
        mesh=mesh,
        in_specs=placed,
        out_specs=(
            P(("depth", "col"), "row"),
            P("row", ("col", "depth")),
            P("col", ("row", "depth")),
        ),
        check_vma=False,
    )
```
